32 devices in a mesh: span: 8 (over z, x), chord: 4 (over y, core).
Axes of the slice: x: 2, y: 2, z: 4, core: 2. Of those that a mesh axis runs over, the one named last changes fastest.
Arguments:
- pressure: float32 [2, 1024, 512], P(None, 'span', 'chord'), may hold values from 0 to 1
- fill_state: int32 [2, 1024, 512], P(None, 'span', 'chord'), may hold values from 0 to 2
- perm_class: int32 [2, 1024, 512], P(None, 'span', 'chord'), may hold values from 0 to 7
- perm_table: float32 [2, 8], replicated, may hold values from 1 to 4
- inlet_span: int32 [128], replicated, may hold values from 0 to 1023
- inlet_chord: int32 [128], replicated, may hold values from 0 to 511
- inlet_rate: float32 [128], replicated, may hold values from 500 to 1500
Outputs:
- pressure_out: float32 [2, 1024, 512], P(None, 'span', 'chord')
The draws below stay inside these ranges and needn't reach their ends.
Inputs may be any that keep to these rules, and one draw needn't show every extreme that they name: `inlet_span`: inlet cells may repeat; their rates add.
All inputs are finite; a program needn't handle non-finite values.
Results may differ from the reference program's by a relative error of at most 0.00035.
Values sent between devices are 32-bit elements; how exact they have to be, the bound alone decides.
A program may use at most 64 MiB of HBM per device.

```python
import math
import jax
import jax.numpy as jnp

PLIES = 2
STEPS = 1
NCLASS = 8
NIN = 128
NS = 1024
NC = 512


def plant(result, own_key, least, high):
    shape = result.shape
    index_at = [jax.random.randint(jax.random.fold_in(own_key, axis), (), 0, shape[axis]) for axis in range(len(shape))]
    result = result.at[tuple(index_at)].set(least)
    longest = shape.index(max(shape))
    index_at[longest] = (index_at[longest] + 1) % shape[longest]
    return result.at[tuple(index_at)].set(high)


def block_scale(rng, extent, cuts, smallest, high):
    def one(axis_at, blocks):
        steps = jax.random.uniform(jax.random.fold_in(jax.random.fold_in(rng, 6), axis_at), (blocks,), jnp.float32, smallest / len(cuts), high / len(cuts))
        return jnp.repeat(jnp.exp(steps), extent[axis_at] // blocks).reshape((-1,) + (1,) * (len(extent) - axis_at - 1))

    loudness = one(*cuts[0])
    for cut in cuts[1:]:
        loudness = loudness * one(*cut)
    return loudness


def setup_inputs(seed: int = 0) -> dict:
    key_of = jax.random.split(jax.random.key(seed), 8)
    pressure = jnp.clip(1.0 * jax.random.uniform(key_of[0], (PLIES, NS, NC), jnp.float32) ** block_scale(key_of[0], (PLIES, NS, NC), ((1, 8), (2, 4)), -0.2, 0.2), 0.0, 1.0)
    fill_state = plant(jax.random.randint(key_of[1], (PLIES, NS, NC), 0, 3), jax.random.fold_in(key_of[1], 1), 0, 2).astype(jnp.int32)
    perm_class = plant(jax.random.randint(key_of[2], (PLIES, NS, NC), 0, NCLASS), jax.random.fold_in(key_of[2], 1), 0, NCLASS - 1).astype(jnp.int32)
    perm_table = jnp.clip(jnp.exp(jax.random.uniform(key_of[3], (PLIES, NCLASS), jnp.float32, math.log(1.0), math.log(4.0))), 1.0, 4.0)
    inlet_span = plant(jax.random.randint(key_of[4], (NIN,), 0, NS), jax.random.fold_in(key_of[4], 1), 0, NS - 1).astype(jnp.int32)
    inlet_chord = plant(jax.random.randint(key_of[5], (NIN,), 0, NC), jax.random.fold_in(key_of[5], 1), 0, NC - 1).astype(jnp.int32)
    inlet_rate = jnp.clip(jax.random.uniform(key_of[6], (NIN,), jnp.float32, 500.0, 1500.0), 500.0, 1500.0)
    return {"pressure": pressure, "fill_state": fill_state, "perm_class": perm_class, "perm_table": perm_table, "inlet_span": inlet_span, "inlet_chord": inlet_chord, "inlet_rate": inlet_rate}


HALF_RATE = 200.0
COUPLE = 0.3


def shift_lower(values, stride):
    padding = jnp.zeros(values.shape[:-1] + (stride,), values.dtype)
    return jnp.concatenate([padding, values[..., :-stride]], axis=-1)


def shift_upper(values, stride):
    padding = jnp.zeros(values.shape[:-1] + (stride,), values.dtype)
    return jnp.concatenate([values[..., stride:], padding], axis=-1)


def faces(cond):
    summed = HALF_RATE * (cond + shift_upper(cond, 1))
    closing = jnp.zeros(cond.shape[:-1] + (1,), cond.dtype)
    return jnp.concatenate([summed[..., :-1], closing], axis=-1)


def parallel_cyclic_reduction_update(lower_band, diagonal_terms, upper_band, right_hand_side, previous_neighbour_row, next_neighbour_row):
    new_lower = -lower_band * previous_neighbour_row[0]
    new_diag = diagonal_terms - lower_band * previous_neighbour_row[1] - upper_band * next_neighbour_row[0]
    new_upper = -upper_band * next_neighbour_row[1]
    new_rhs = right_hand_side - lower_band * previous_neighbour_row[2] - upper_band * next_neighbour_row[2]
    return new_lower, new_diag, new_upper, new_rhs


def line_solve(lower_band, diagonal_terms, upper_band, right_hand_side):
    total = right_hand_side.shape[-1]
    stride = 1
    while stride < total:
        ratios = (lower_band / diagonal_terms, upper_band / diagonal_terms, right_hand_side / diagonal_terms)
        previous_neighbour_row = [shift_lower(v, stride) for v in ratios]
        next_neighbour_row = [shift_upper(v, stride) for v in ratios]
        lower_band, diagonal_terms, upper_band, right_hand_side = parallel_cyclic_reduction_update(lower_band, diagonal_terms, upper_band, right_hand_side, previous_neighbour_row, next_neighbour_row)
        stride = stride * 2
    return right_hand_side / diagonal_terms


def explicit_core(field, field_next, field_prev, faces_here, faces_prev, source):
    flux = faces_here * (field_next - field) - faces_prev * (field - field_prev)
    return field + flux + COUPLE * (jnp.flip(field, 0) - field) + source


def second_half(star, half_lines, source):
    return 2.0 * star - half_lines + COUPLE * (jnp.flip(star, 0) - star) + source


def reference(pressure, fill_state, perm_class, perm_table, inlet_span, inlet_chord, inlet_rate):
    mobility = jnp.where(fill_state == 0, 1.0, jnp.where(fill_state == 1, 0.5, 0.25))
    plies_idx = jnp.arange(PLIES, dtype=jnp.int32)[:, None, None]
    cond = perm_table[plies_idx, perm_class] * mobility
    plane = jnp.zeros((NS, NC), jnp.float32).at[inlet_span, inlet_chord].add(inlet_rate)
    source = jnp.broadcast_to(plane[None], (PLIES, NS, NC))
    source_turned = jnp.transpose(source, (0, 2, 1))
    chord_faces = faces(cond)
    chord_prev = shift_lower(chord_faces, 1)
    span_faces = faces(jnp.transpose(cond, (0, 2, 1)))
    span_prev = shift_lower(span_faces, 1)
    field = pressure
    for step in range(STEPS):
        half = explicit_core(field, shift_upper(field, 1), shift_lower(field, 1), chord_faces, chord_prev, source)
        half_turned = jnp.transpose(half, (0, 2, 1))
        star = line_solve(-span_prev, 1.0 + span_prev + span_faces, -span_faces, half_turned)
        second = second_half(star, half_turned, source_turned)
        field = line_solve(-chord_prev, 1.0 + chord_prev + chord_faces, -chord_faces, jnp.transpose(second, (0, 2, 1)))
    return field
```

```python
import functools

import jax
import jax.numpy as jnp
from jax import lax
from jax.experimental import pallas as pl
from jax.experimental.pallas import tpu as pltpu
from jax.sharding import PartitionSpec as P

HALF_RATE = 200.0
COUPLE = 0.3
MESH = pl.DeviceIdType.MESH
TILE = 8


def down(x, s):
    if s % TILE == 0:
        return jnp.concatenate([x[-s:], x[:-s]], axis=0)
    return pltpu.roll(x, s, 0)


def up(x, s):
    if s % TILE == 0:
        return jnp.concatenate([x[s:], x[:s]], axis=0)
    return pltpu.roll(x, x.shape[0] - s, 0)


def from_row(s, value, other):
    if s % TILE == 0:
        return jnp.concatenate([other[:s], value[s:]], axis=0)
    rows = lax.broadcasted_iota(jnp.int32, value.shape, 0)
    return jnp.where(rows >= s, value, other)


def to_row(s, value, other):
    n = value.shape[0]
    if s % TILE == 0:
        return jnp.concatenate([value[: n - s], other[n - s :]], axis=0)
    rows = lax.broadcasted_iota(jnp.int32, value.shape, 0)
    return jnp.where(rows < n - s, value, other)


def factor(cond, keep):
    n = cond.shape[0]
    zero = jnp.zeros_like(cond)
    one = jnp.ones_like(cond)
    g = HALF_RATE * (cond + up(cond, 1))
    a = from_row(1, down(g, 1), one)
    c = to_row(1, g, one)
    e = one
    s, k = 1, 0
    while s < n:
        a_in = from_row(s, a, zero)
        c_in = to_row(s, c, zero)
        rb = 1.0 / (e + a_in + c_in)
        al = a_in * down(rb, s)
        be = c_in * up(rb, s)
        keep(k, al, be)
        a = from_row(s, al * down(a, s), a)
        c = to_row(s, be * up(c, s), c)
        e = e + al * down(e, s) + be * up(e, s)
        s, k = 2 * s, k + 1
    re = 1.0 / e
    return a * re, c * re, re


def reduce_rhs(d, kept, re):
    n = d.shape[0]
    s, k = 1, 0
    while s < n:
        al, be = kept(k)
        if s % TILE == 0:
            zero = jnp.zeros_like(d[:s])
            d = (
                d
                + jnp.concatenate([zero, al[s:] * d[:-s]], axis=0)
                + jnp.concatenate([be[:-s] * d[s:], zero], axis=0)
            )
        else:
            d = d + al * down(d, s) + be * up(d, s)
        s, k = 2 * s, k + 1
    return d * re


class Gather:
    def __init__(self, axis, n, me, buf, send, recv):
        self.copies = []
        self.landed = []
        for o in range(1, n):
            dst = lax.rem(me + o, n)
            src = lax.rem(me + n - o, n)
            self.copies.append(
                pltpu.make_async_remote_copy(
                    buf.at[me], buf.at[me], send.at[o], recv.at[o], {axis: dst}, MESH
                )
            )
            self.landed.append(
                pltpu.make_async_remote_copy(
                    buf.at[src], buf.at[src], send.at[o], recv.at[o], {axis: dst}, MESH
                )
            )

    def start(self):
        for copy in self.copies:
            copy.start()

    def wait(self):
        for copy in self.landed:
            copy.wait_recv()

    def wait_sent(self):
        for copy in self.copies:
            copy.wait_send()


def put_coefs(buf, me, plies, p, A, C, cond):
    n = A.shape[0]
    values = (A[:1], C[n - 1 :], A[n - 1 :], cond[:1], cond[n - 1 :])
    for q, v in enumerate(values):
        buf[me, q * plies + p : q * plies + p + 1, :] = v


def flux_factor(buf, n, plies):
    def at(j, q):
        return buf[j, q * plies : (q + 1) * plies, :]

    w, m = [None] * (n + 1), [None] * (n + 1)
    cross = [at(j, 2) for j in range(n)]
    for j in range(1, n):
        diag = 1.0 / (HALF_RATE * (at(j - 1, 4) + at(j, 3))) + at(j - 1, 1) + at(j, 0)
        if j > 1:
            m[j] = cross[j - 1] * w[j - 1]
            diag = diag - cross[j - 1] * m[j]
        w[j] = 1.0 / diag
    return w, m, cross


def flux_solve(buf, n, plies, me, w, m, cross):
    y = [None] * (n + 1)
    for j in range(1, n):
        r = buf[j - 1, plies : 2 * plies, :] - buf[j, :plies, :]
        y[j] = r if j == 1 else r + m[j] * y[j - 1]
    zero = jnp.zeros((plies, buf.shape[-1]), jnp.float32)
    top, bottom = zero, zero
    flux = None
    for j in range(n - 1, 0, -1):
        flux = w[j] * (y[j] if flux is None else y[j] + cross[j] * flux)
        top = jnp.where(me == j, flux, top)
        bottom = jnp.where(me + 1 == j, flux, bottom)
    return top, bottom


def kernel(
    ns, nc, plies, classes,
    pressure_hbm, fill_hbm, class_hbm, table_ref, span_ref, chord_ref, rate_ref,
    out_ref,
    pressure, fill, klass, half, keep_s, keep_c, A_s, C_s, E_s, A_c, C_c, E_c, D,
    halo_out, halo_in, coef_s, coef_c, edge_s, edge_c,
    load_sem, halo_send, halo_recv,
    cs_send, cs_recv, cc_send, cc_recv, es_send, es_recv, ec_send, ec_recv,
):
    rows, width = pressure.shape[1:]
    me_s, me_c = lax.axis_index("span"), lax.axis_index("chord")
    barrier = pltpu.get_barrier_semaphore()
    for o in range(1, nc):
        pl.semaphore_signal(
            barrier, inc=1, device_id={"chord": lax.rem(me_c + o, nc)}, device_id_type=MESH
        )
    for o in range(1, ns):
        pl.semaphore_signal(
            barrier, inc=1, device_id={"span": lax.rem(me_s + o, ns)}, device_id_type=MESH
        )
    loads = [
        pltpu.make_async_copy(src, dst, load_sem.at[i])
        for i, (src, dst) in enumerate(
            ((class_hbm, klass), (fill_hbm, fill), (pressure_hbm, pressure))
        )
    ]
    for load in loads:
        load.start()

    row_id = lax.broadcasted_iota(jnp.int32, (rows, span_ref.shape[1]), 0) + me_s * rows
    col_id = lax.broadcasted_iota(jnp.int32, (width, span_ref.shape[1]), 0) + me_c * width
    row_hits = jnp.where(row_id == span_ref[...], rate_ref[...], 0.0)
    col_hits = jnp.where(col_id == chord_ref[...], 1.0, 0.0)
    plane = lax.dot_general(
        row_hits, col_hits, (((1,), (1,)), ((), ())),
        precision=lax.Precision.HIGHEST, preferred_element_type=jnp.float32,
    )

    for load in loads:
        load.wait()

    conds, turned, fields = [], [], []
    for p in range(plies):
        perm = jnp.full((rows, width), table_ref[p, 0], jnp.float32)
        kl = klass[p]
        for k in range(1, classes):
            perm = jnp.where(kl == k, table_ref[p, k], perm)
        st = fill[p]
        cond = perm * jnp.where(st == 0, 1.0, jnp.where(st == 1, 0.5, 0.25))
        conds.append(cond)
        turned.append(cond.T)
        fields.append(pressure[p].T)
        for side, at in ((0, 0), (1, width - 1)):
            halo_out[side, p : p + 1, :] = turned[p][at : at + 1]
            halo_out[side, plies + p : plies + p + 1, :] = fields[p][at : at + 1]

    pl.semaphore_wait(barrier, ns + nc - 2)
    ahead, behind = lax.rem(me_c + 1, nc), lax.rem(me_c + nc - 1, nc)
    halos = [
        pltpu.make_async_remote_copy(
            halo_out.at[side], halo_in.at[side], halo_send.at[side], halo_recv.at[side],
            {"chord": to}, MESH,
        )
        for side, to in ((0, behind), (1, ahead))
    ]
    for copy in halos:
        copy.start()

    def keeper(ref, p):
        def keep(k, al, be):
            ref[k, 0, p] = al
            ref[k, 1, p] = be

        return keep

    def kept(ref, p):
        return lambda k: (ref[k, 0, p], ref[k, 1, p])

    for p in range(plies):
        A, C, re = factor(conds[p], keeper(keep_s, p))
        A_s[p], C_s[p], E_s[p] = A, C, re
        put_coefs(coef_s, me_s, plies, p, A, C, conds[p])
    span_coefs = Gather("span", ns, me_s, coef_s, cs_send, cs_recv)
    span_coefs.start()

    explicit = []
    for p in range(plies):
        f, other = fields[p], fields[plies - 1 - p]
        g = HALF_RATE * (turned[p] + up(turned[p], 1))
        flow = to_row(1, g * (up(f, 1) - f), jnp.zeros_like(f))
        back = from_row(1, down(flow, 1), jnp.zeros_like(f))
        explicit.append(f + (flow - back) + COUPLE * (other - f))

    for copy in halos:
        copy.wait_recv()
    lanes = lax.broadcasted_iota(jnp.int32, (width, rows), 0)
    for p in range(plies):
        behind_c, behind_f = halo_in[1, p : p + 1, :], halo_in[1, plies + p : plies + p + 1, :]
        ahead_c, ahead_f = halo_in[0, p : p + 1, :], halo_in[0, plies + p : plies + p + 1, :]
        first = HALF_RATE * (behind_c + turned[p][:1]) * (behind_f - fields[p][:1])
        last = HALF_RATE * (ahead_c + turned[p][width - 1 :]) * (ahead_f - fields[p][width - 1 :])
        first = jnp.where(me_c > 0, first, 0.0)
        last = jnp.where(me_c < nc - 1, last, 0.0)
        total = (
            explicit[p]
            + jnp.where(lanes == 0, first, 0.0)
            + jnp.where(lanes == width - 1, last, 0.0)
        )
        rhs = total.T + plane
        half[p] = rhs
        d = reduce_rhs(rhs, kept(keep_s, p), E_s[p])
        D[p] = d
        edge_s[me_s, p : p + 1, :] = d[:1]
        edge_s[me_s, plies + p : plies + p + 1, :] = d[rows - 1 :]
    span_edges = Gather("span", ns, me_s, edge_s, es_send, es_recv)
    span_edges.start()

    for p in range(plies):
        A, C, re = factor(turned[p], keeper(keep_c, p))
        A_c[p], C_c[p], E_c[p] = A, C, re
        put_coefs(coef_c, me_c, plies, p, A, C, turned[p])
    chord_coefs = Gather("chord", nc, me_c, coef_c, cc_send, cc_recv)
    chord_coefs.start()

    span_coefs.wait()
    parts = flux_factor(coef_s, ns, plies)
    span_edges.wait()
    top, bottom = flux_solve(edge_s, ns, plies, me_s, *parts)
    stars = [D[p] + A_s[p] * top[p : p + 1] - C_s[p] * bottom[p : p + 1] for p in range(plies)]
    for p in range(plies):
        star, other = stars[p], stars[plies - 1 - p]
        second = 2.0 * star - half[p] + COUPLE * (other - star) + plane
        d = reduce_rhs(second.T, kept(keep_c, p), E_c[p])
        D[p] = d
        edge_c[me_c, p : p + 1, :] = d[:1]
        edge_c[me_c, plies + p : plies + p + 1, :] = d[width - 1 :]
    chord_edges = Gather("chord", nc, me_c, edge_c, ec_send, ec_recv)
    chord_edges.start()

    chord_coefs.wait()
    parts = flux_factor(coef_c, nc, plies)
    chord_edges.wait()
    top, bottom = flux_solve(edge_c, nc, plies, me_c, *parts)
    for p in range(plies):
        line = D[p] + A_c[p] * top[p : p + 1] - C_c[p] * bottom[p : p + 1]
        out_ref[p] = line.T

    for copy in halos:
        copy.wait_send()
    for gather in (span_coefs, chord_coefs, span_edges, chord_edges):
        gather.wait_sent()


def levels(n):
    return max(1, (n - 1).bit_length())


def per_device(ns, nc, pressure, fill_state, perm_class, perm_table, inlet_span, inlet_chord, inlet_rate):
    plies, rows, width = pressure.shape
    classes = perm_table.shape[1]
    inlets = inlet_span.shape[0]
    vmem = pl.BlockSpec(memory_space=pltpu.VMEM)
    hbm = pl.BlockSpec(memory_space=pl.ANY)
    smem = pl.BlockSpec(memory_space=pltpu.SMEM)
    f32 = jnp.float32
    block = pltpu.VMEM((plies, rows, width), f32)
    block_t = pltpu.VMEM((plies, width, rows), f32)
    iblock = pltpu.VMEM((plies, rows, width), jnp.int32)
    pad = lambda n: -(-n // TILE) * TILE
    dma = lambda n: pltpu.SemaphoreType.DMA((n,))
    return pl.pallas_call(
        functools.partial(kernel, ns, nc, plies, classes),
        out_shape=jax.ShapeDtypeStruct(pressure.shape, f32),
        in_specs=[hbm, hbm, hbm, smem, vmem, vmem, vmem],
        out_specs=vmem,
        scratch_shapes=[
            block, iblock, iblock, block,
            pltpu.VMEM((levels(rows), 2, plies, rows, width), f32),
            pltpu.VMEM((levels(width), 2, plies, width, rows), f32),
            block, block, block, block_t, block_t, block_t, block,
            pltpu.VMEM((2, pad(2 * plies), rows), f32),
            pltpu.VMEM((2, pad(2 * plies), rows), f32),
            pltpu.VMEM((ns, pad(5 * plies), width), f32),
            pltpu.VMEM((nc, pad(5 * plies), rows), f32),
            pltpu.VMEM((ns, pad(2 * plies), width), f32),
            pltpu.VMEM((nc, pad(2 * plies), rows), f32),
            dma(3), dma(2), dma(2),
            dma(ns), dma(ns), dma(nc), dma(nc), dma(ns), dma(ns), dma(nc), dma(nc),
        ],
        compiler_params=pltpu.CompilerParams(collective_id=0, has_side_effects=True),
    )(
        pressure, fill_state, perm_class, perm_table,
        inlet_span.reshape(1, inlets), inlet_chord.reshape(1, inlets), inlet_rate.reshape(1, inlets),
    )


def solution(mesh):
    block = P(None, "span", "chord")
    return jax.shard_map(
        functools.partial(per_device, mesh.shape["span"], mesh.shape["chord"]),
        mesh=mesh,
        in_specs=(block, block, block, P(), P(), P(), P()),
        out_specs=block,
        check_vma=False,
    )
```

```python
import functools

import jax
import jax.numpy as jnp
from jax import lax
from jax.experimental import pallas as pl
from jax.experimental.pallas import tpu as pltpu
from jax.sharding import PartitionSpec as P

HALF_RATE = 200.0
COUPLE = 0.3
MESH = pl.DeviceIdType.MESH
TILE = 8
LIMIT = 16 << 20


def down(x, s):
    if s % TILE == 0:
        return jnp.concatenate([x[-s:], x[:-s]], axis=0)
    return pltpu.roll(x, s, 0)


def up(x, s):
    if s % TILE == 0:
        return jnp.concatenate([x[s:], x[:s]], axis=0)
    return pltpu.roll(x, x.shape[0] - s, 0)


def from_row(s, value, other):
    if s % TILE == 0:
        return jnp.concatenate([other[:s], value[s:]], axis=0)
    rows = lax.broadcasted_iota(jnp.int32, value.shape, 0)
    return jnp.where(rows >= s, value, other)


def to_row(s, value, other):
    n = value.shape[0]
    if s % TILE == 0:
        return jnp.concatenate([value[: n - s], other[n - s :]], axis=0)
    rows = lax.broadcasted_iota(jnp.int32, value.shape, 0)
    return jnp.where(rows < n - s, value, other)


def factor(cond, keep):
    n = cond.shape[0]
    zero = jnp.zeros_like(cond)
    one = jnp.ones_like(cond)
    g = HALF_RATE * (cond + up(cond, 1))
    a = from_row(1, down(g, 1), one)
    c = to_row(1, g, one)
    e = one
    s, k = 1, 0
    while s < n:
        a_in = from_row(s, a, zero)
        c_in = to_row(s, c, zero)
        rb = 1.0 / (e + a_in + c_in)
        al = a_in * down(rb, s)
        be = c_in * up(rb, s)
        keep(k, al, be)
        a = from_row(s, al * down(a, s), a)
        c = to_row(s, be * up(c, s), c)
        e = e + al * down(e, s) + be * up(e, s)
        s, k = 2 * s, k + 1
    re = 1.0 / e
    return a * re, c * re, re


def reduce_rhs(d, kept, re):
    n = d.shape[0]
    s, k = 1, 0
    while s < n:
        al, be = kept(k)
        if s % TILE == 0:
            zero = jnp.zeros_like(d[:s])
            d = (
                d
                + jnp.concatenate([zero, al[s:] * d[:-s]], axis=0)
                + jnp.concatenate([be[:-s] * d[s:], zero], axis=0)
            )
        else:
            d = d + al * down(d, s) + be * up(d, s)
        s, k = 2 * s, k + 1
    return d * re


class Gather:
    def __init__(self, axis, n, me, buf, send, recv):
        self.copies = []
        self.landed = []
        for o in range(1, n):
            dst = lax.rem(me + o, n)
            src = lax.rem(me + n - o, n)
            self.copies.append(
                pltpu.make_async_remote_copy(
                    buf.at[me], buf.at[me], send.at[o], recv.at[o], {axis: dst}, MESH
                )
            )
            self.landed.append(
                pltpu.make_async_remote_copy(
                    buf.at[src], buf.at[src], send.at[o], recv.at[o], {axis: dst}, MESH
                )
            )

    def start(self):
        for copy in self.copies:
            copy.start()

    def wait(self):
        for copy in self.landed:
            copy.wait_recv()

    def wait_sent(self):
        for copy in self.copies:
            copy.wait_send()


def put_coefs(buf, me, plies, p, A, C, cond):
    n = A.shape[0]
    values = (A[:1], C[n - 1 :], A[n - 1 :], cond[:1], cond[n - 1 :])
    for q, v in enumerate(values):
        buf[me, q * plies + p : q * plies + p + 1, :] = v


def flux_factor(buf, n, plies):
    def at(j, q):
        return buf[j, q * plies : (q + 1) * plies, :]

    w, m = [None] * (n + 1), [None] * (n + 1)
    cross = [at(j, 2) for j in range(n)]
    for j in range(1, n):
        diag = 1.0 / (HALF_RATE * (at(j - 1, 4) + at(j, 3))) + at(j - 1, 1) + at(j, 0)
        if j > 1:
            m[j] = cross[j - 1] * w[j - 1]
            diag = diag - cross[j - 1] * m[j]
        w[j] = 1.0 / diag
    return w, m, cross


def flux_solve(buf, n, plies, me, w, m, cross):
    y = [None] * (n + 1)
    for j in range(1, n):
        r = buf[j - 1, plies : 2 * plies, :] - buf[j, :plies, :]
        y[j] = r if j == 1 else r + m[j] * y[j - 1]
    zero = jnp.zeros((plies, buf.shape[-1]), jnp.float32)
    top, bottom = zero, zero
    flux = None
    for j in range(n - 1, 0, -1):
        flux = w[j] * (y[j] if flux is None else y[j] + cross[j] * flux)
        top = jnp.where(me == j, flux, top)
        bottom = jnp.where(me + 1 == j, flux, bottom)
    return top, bottom


def kernel(
    ns, nc, plies, classes,
    pressure_hbm, fill_hbm, class_hbm, table_hbm, span_hbm, chord_hbm, rate_hbm,
    out_ref,
    pressure, fill, klass, table_ref, span_ref, chord_ref, rate_ref, half, keep_s, keep_c, A_s, C_s, E_s, A_c, C_c, E_c, D,
    halo_out, halo_in, coef_s, coef_c, edge_s, edge_c,
    load_sem, halo_send, halo_recv,
    cs_send, cs_recv, cc_send, cc_recv, es_send, es_recv, ec_send, ec_recv,
):
    rows, width = pressure.shape[1:]
    me_s, me_c = lax.axis_index("span"), lax.axis_index("chord")
    barrier = pltpu.get_barrier_semaphore()
    for o in range(1, nc):
        pl.semaphore_signal(
            barrier, inc=1, device_id={"chord": lax.rem(me_c + o, nc)}, device_id_type=MESH
        )
    for o in range(1, ns):
        pl.semaphore_signal(
            barrier, inc=1, device_id={"span": lax.rem(me_s + o, ns)}, device_id_type=MESH
        )
    loads = [
        pltpu.make_async_copy(src, dst, load_sem.at[i])
        for i, (src, dst) in enumerate(
            (
                (class_hbm, klass), (fill_hbm, fill), (pressure_hbm, pressure), (table_hbm, table_ref),
                (span_hbm, span_ref), (chord_hbm, chord_ref), (rate_hbm, rate_ref),
            )
        )
    ]
    for load in loads:
        load.start()

    for load in loads:
        load.wait()

    conds, turned, fields = [], [], []
    for p in range(plies):
        perm = jnp.full((rows, width), table_ref[p, 0], jnp.float32)
        kl = klass[p]
        for k in range(1, classes):
            perm = jnp.where(kl == k, table_ref[p, k], perm)
        st = fill[p]
        cond = perm * jnp.where(st == 0, 1.0, jnp.where(st == 1, 0.5, 0.25))
        conds.append(cond)
        turned.append(cond.T)
        fields.append(pressure[p].T)
        for side, at in ((0, 0), (1, width - 1)):
            halo_out[side, p : p + 1, :] = turned[p][at : at + 1]
            halo_out[side, plies + p : plies + p + 1, :] = fields[p][at : at + 1]

    pl.semaphore_wait(barrier, ns + nc - 2)
    ahead, behind = lax.rem(me_c + 1, nc), lax.rem(me_c + nc - 1, nc)
    halos = [
        pltpu.make_async_remote_copy(
            halo_out.at[side], halo_in.at[side], halo_send.at[side], halo_recv.at[side],
            {"chord": to}, MESH,
        )
        for side, to in ((0, behind), (1, ahead))
    ]
    for copy in halos:
        copy.start()

    def keeper(ref, p):
        def keep(k, al, be):
            ref[k, 0, p] = al
            ref[k, 1, p] = be

        return keep

    def kept(ref, p):
        return lambda k: (ref[k, 0, p], ref[k, 1, p])

    for p in range(plies):
        A, C, re = factor(conds[p], keeper(keep_s, p))
        A_s[p], C_s[p], E_s[p] = A, C, re
        put_coefs(coef_s, me_s, plies, p, A, C, conds[p])
    span_coefs = Gather("span", ns, me_s, coef_s, cs_send, cs_recv)
    span_coefs.start()

    row_id = lax.broadcasted_iota(jnp.int32, (rows, span_ref.shape[1]), 0) + me_s * rows
    col_id = lax.broadcasted_iota(jnp.int32, (width, span_ref.shape[1]), 0) + me_c * width
    row_hits = jnp.where(row_id == span_ref[...], rate_ref[...], 0.0)
    col_hits = jnp.where(col_id == chord_ref[...], 1.0, 0.0)
    plane = lax.dot_general(
        row_hits, col_hits, (((1,), (1,)), ((), ())),
        precision=lax.Precision.HIGHEST, preferred_element_type=jnp.float32,
    )

    explicit = []
    for p in range(plies):
        f, other = fields[p], fields[plies - 1 - p]
        g = HALF_RATE * (turned[p] + up(turned[p], 1))
        flow = to_row(1, g * (up(f, 1) - f), jnp.zeros_like(f))
        back = from_row(1, down(flow, 1), jnp.zeros_like(f))
        explicit.append(f + (flow - back) + COUPLE * (other - f))

    for copy in halos:
        copy.wait_recv()
    lanes = lax.broadcasted_iota(jnp.int32, (width, rows), 0)
    for p in range(plies):
        behind_c, behind_f = halo_in[1, p : p + 1, :], halo_in[1, plies + p : plies + p + 1, :]
        ahead_c, ahead_f = halo_in[0, p : p + 1, :], halo_in[0, plies + p : plies + p + 1, :]
        first = HALF_RATE * (behind_c + turned[p][:1]) * (behind_f - fields[p][:1])
        last = HALF_RATE * (ahead_c + turned[p][width - 1 :]) * (ahead_f - fields[p][width - 1 :])
        first = jnp.where(me_c > 0, first, 0.0)
        last = jnp.where(me_c < nc - 1, last, 0.0)
        total = (
            explicit[p]
            + jnp.where(lanes == 0, first, 0.0)
            + jnp.where(lanes == width - 1, last, 0.0)
        )
        rhs = total.T + plane
        half[p] = rhs
        d = reduce_rhs(rhs, kept(keep_s, p), E_s[p])
        D[p] = d
        edge_s[me_s, p : p + 1, :] = d[:1]
        edge_s[me_s, plies + p : plies + p + 1, :] = d[rows - 1 :]
    span_edges = Gather("span", ns, me_s, edge_s, es_send, es_recv)
    span_edges.start()

    for p in range(plies):
        A, C, re = factor(turned[p], keeper(keep_c, p))
        A_c[p], C_c[p], E_c[p] = A, C, re
        put_coefs(coef_c, me_c, plies, p, A, C, turned[p])
    chord_coefs = Gather("chord", nc, me_c, coef_c, cc_send, cc_recv)
    chord_coefs.start()

    span_coefs.wait()
    parts = flux_factor(coef_s, ns, plies)
    span_edges.wait()
    top, bottom = flux_solve(edge_s, ns, plies, me_s, *parts)
    stars = [D[p] + A_s[p] * top[p : p + 1] - C_s[p] * bottom[p : p + 1] for p in range(plies)]
    for p in range(plies):
        star, other = stars[p], stars[plies - 1 - p]
        second = 2.0 * star - half[p] + COUPLE * (other - star) + plane
        d = reduce_rhs(second.T, kept(keep_c, p), E_c[p])
        D[p] = d
        edge_c[me_c, p : p + 1, :] = d[:1]
        edge_c[me_c, plies + p : plies + p + 1, :] = d[width - 1 :]
    chord_edges = Gather("chord", nc, me_c, edge_c, ec_send, ec_recv)
    chord_edges.start()

    chord_coefs.wait()
    parts = flux_factor(coef_c, nc, plies)
    chord_edges.wait()
    top, bottom = flux_solve(edge_c, nc, plies, me_c, *parts)
    for p in range(plies):
        line = D[p] + A_c[p] * top[p : p + 1] - C_c[p] * bottom[p : p + 1]
        out_ref[p] = line.T

    for copy in halos:
        copy.wait_send()
    for gather in (span_coefs, chord_coefs, span_edges, chord_edges):
        gather.wait_sent()


def levels(n):
    return max(1, (n - 1).bit_length())


def per_device(ns, nc, pressure, fill_state, perm_class, perm_table, inlet_span, inlet_chord, inlet_rate):
    plies, rows, width = pressure.shape
    classes = perm_table.shape[1]
    inlets = inlet_span.shape[0]
    vmem = pl.BlockSpec(memory_space=pltpu.VMEM)
    hbm = pl.BlockSpec(memory_space=pltpu.HBM)
    f32 = jnp.float32
    block = pltpu.VMEM((plies, rows, width), f32)
    block_t = pltpu.VMEM((plies, width, rows), f32)
    iblock = pltpu.VMEM((plies, rows, width), jnp.int32)
    dma = lambda n: pltpu.SemaphoreType.DMA((n,))
    return pl.pallas_call(
        functools.partial(kernel, ns, nc, plies, classes),
        out_shape=pltpu.VMEM(pressure.shape, f32),
        in_specs=[hbm] * 7,
        out_specs=vmem,
        scratch_shapes=[
            block, iblock, iblock,
            pltpu.SMEM(perm_table.shape, f32),
            pltpu.VMEM((1, inlets), jnp.int32), pltpu.VMEM((1, inlets), jnp.int32), pltpu.VMEM((1, inlets), f32),
            block,
            pltpu.VMEM((levels(rows), 2, plies, rows, width), f32),
            pltpu.VMEM((levels(width), 2, plies, width, rows), f32),
            block, block, block, block_t, block_t, block_t, block,
            pltpu.VMEM((2, 2 * plies, rows), f32),
            pltpu.VMEM((2, 2 * plies, rows), f32),
            pltpu.VMEM((ns, 5 * plies, width), f32),
            pltpu.VMEM((nc, 5 * plies, rows), f32),
            pltpu.VMEM((ns, 2 * plies, width), f32),
            pltpu.VMEM((nc, 2 * plies, rows), f32),
            dma(7), dma(2), dma(2),
            dma(ns), dma(ns), dma(nc), dma(nc), dma(ns), dma(ns), dma(nc), dma(nc),
        ],
        compiler_params=pltpu.CompilerParams(collective_id=0, has_side_effects=True, vmem_limit_bytes=LIMIT),
    )(
        *(
            pltpu.with_memory_space_constraint(x, pltpu.HBM)
            for x in (
                pressure, fill_state, perm_class, perm_table, inlet_span.reshape(1, inlets),
                inlet_chord.reshape(1, inlets), inlet_rate.reshape(1, inlets),
            )
        )
    )


def solution(mesh):
    block = P(None, "span", "chord")
    return jax.shard_map(
        functools.partial(per_device, mesh.shape["span"], mesh.shape["chord"]),
        mesh=mesh,
        in_specs=(block, block, block, P(), P(), P(), P()),
        out_specs=block,
        check_vma=False,
    )
```

```python
import functools

import jax
import jax.numpy as jnp
from jax import lax
from jax.experimental import pallas as pl
from jax.experimental.pallas import tpu as pltpu
from jax.sharding import PartitionSpec as P

HALF_RATE = 200.0
COUPLE = 0.3
MESH = pl.DeviceIdType.MESH
TILE = 8
LIMIT = 16 << 20


def down(x, s):
    if s % TILE == 0:
        return jnp.concatenate([x[-s:], x[:-s]], axis=0)
    return pltpu.roll(x, s, 0)


def up(x, s):
    if s % TILE == 0:
        return jnp.concatenate([x[s:], x[:s]], axis=0)
    return pltpu.roll(x, x.shape[0] - s, 0)


def from_row(s, value, other):
    if s % TILE == 0:
        return jnp.concatenate([other[:s], value[s:]], axis=0)
    rows = lax.broadcasted_iota(jnp.int32, value.shape, 0)
    return jnp.where(rows >= s, value, other)


def to_row(s, value, other):
    n = value.shape[0]
    if s % TILE == 0:
        return jnp.concatenate([value[: n - s], other[n - s :]], axis=0)
    rows = lax.broadcasted_iota(jnp.int32, value.shape, 0)
    return jnp.where(rows < n - s, value, other)


def factor(cond, keep):
    n = cond.shape[0]
    zero = jnp.zeros_like(cond)
    one = jnp.ones_like(cond)
    g = HALF_RATE * (cond + up(cond, 1))
    a = from_row(1, down(g, 1), one)
    c = to_row(1, g, one)
    e = one
    s, k = 1, 0
    while s < n:
        a_in = from_row(s, a, zero)
        c_in = to_row(s, c, zero)
        rb = 1.0 / (e + a_in + c_in)
        al = a_in * down(rb, s)
        be = c_in * up(rb, s)
        keep(k, al, be)
        a = from_row(s, al * down(a, s), a)
        c = to_row(s, be * up(c, s), c)
        e = e + al * down(e, s) + be * up(e, s)
        s, k = 2 * s, k + 1
    re = 1.0 / e
    return a * re, c * re, re


def reduce_rhs(d, kept, re):
    n = d.shape[0]
    s, k = 1, 0
    while s < n:
        al, be = kept(k)
        if s % TILE == 0:
            zero = jnp.zeros_like(d[:s])
            d = (
                d
                + jnp.concatenate([zero, al[s:] * d[:-s]], axis=0)
                + jnp.concatenate([be[:-s] * d[s:], zero], axis=0)
            )
        else:
            d = d + al * down(d, s) + be * up(d, s)
        s, k = 2 * s, k + 1
    return d * re


class Gather:
    def __init__(self, axis, n, me, buf, send, recv):
        self.copies = []
        self.landed = []
        for o in range(1, n):
            dst = lax.rem(me + o, n)
            src = lax.rem(me + n - o, n)
            self.copies.append(
                pltpu.make_async_remote_copy(
                    buf.at[me], buf.at[me], send.at[o], recv.at[o], {axis: dst}, MESH
                )
            )
            self.landed.append(
                pltpu.make_async_remote_copy(
                    buf.at[src], buf.at[src], send.at[o], recv.at[o], {axis: dst}, MESH
                )
            )

    def start(self):
        for copy in self.copies:
            copy.start()

    def wait(self):
        for copy in self.landed:
            copy.wait_recv()

    def wait_sent(self):
        for copy in self.copies:
            copy.wait_send()


def put_coefs(buf, me, plies, p, A, C, cond):
    n = A.shape[0]
    values = (A[:1], C[n - 1 :], A[n - 1 :], cond[:1], cond[n - 1 :])
    for q, v in enumerate(values):
        buf[me, q * plies + p : q * plies + p + 1, :] = v


def flux_factor(buf, n, plies):
    def at(j, q):
        return buf[j, q * plies : (q + 1) * plies, :]

    w, m = [None] * (n + 1), [None] * (n + 1)
    cross = [at(j, 2) for j in range(n)]
    for j in range(1, n):
        diag = 1.0 / (HALF_RATE * (at(j - 1, 4) + at(j, 3))) + at(j - 1, 1) + at(j, 0)
        if j > 1:
            m[j] = cross[j - 1] * w[j - 1]
            diag = diag - cross[j - 1] * m[j]
        w[j] = 1.0 / diag
    return w, m, cross


def flux_solve(buf, n, plies, me, w, m, cross):
    y = [None] * (n + 1)
    for j in range(1, n):
        r = buf[j - 1, plies : 2 * plies, :] - buf[j, :plies, :]
        y[j] = r if j == 1 else r + m[j] * y[j - 1]
    zero = jnp.zeros((plies, buf.shape[-1]), jnp.float32)
    top, bottom = zero, zero
    flux = None
    for j in range(n - 1, 0, -1):
        flux = w[j] * (y[j] if flux is None else y[j] + cross[j] * flux)
        top = jnp.where(me == j, flux, top)
        bottom = jnp.where(me + 1 == j, flux, bottom)
    return top, bottom


def kernel(
    ns, nc, plies, classes,
    pressure_hbm, fill_hbm, class_hbm, table_hbm, span_hbm, chord_hbm, rate_hbm,
    out_ref,
    pressure, fill, klass, table_ref, span_ref, chord_ref, rate_ref, half, keep_s, keep_c, A_s, C_s, E_s, A_c, C_c, E_c, D, D_c, sides,
    halo_out, halo_in, coef_s, coef_c, edge_s, edge_c,
    load_sem, halo_send, halo_recv,
    cs_send, cs_recv, cc_send, cc_recv, es_send, es_recv, ec_send, ec_recv,
):
    rows, width = pressure.shape[1:]
    me_s, me_c = lax.axis_index("span"), lax.axis_index("chord")
    barrier = pltpu.get_barrier_semaphore()
    for o in range(1, nc):
        pl.semaphore_signal(
            barrier, inc=1, device_id={"chord": lax.rem(me_c + o, nc)}, device_id_type=MESH
        )
    loads = [
        pltpu.make_async_copy(src, dst, load_sem.at[i])
        for i, (src, dst) in enumerate(
            (
                (class_hbm, klass), (fill_hbm, fill), (pressure_hbm, pressure), (table_hbm, table_ref),
                (span_hbm, span_ref), (chord_hbm, chord_ref), (rate_hbm, rate_ref),
            )
        )
    ]
    for load in loads:
        load.start()
    for o in range(1, ns):
        pl.semaphore_signal(
            barrier, inc=1, device_id={"span": lax.rem(me_s + o, ns)}, device_id_type=MESH
        )

    for load in loads:
        load.wait()

    conds, turned, fields = [], [], []
    for p in range(plies):
        perm = jnp.full((rows, width), table_ref[p, 0], jnp.float32)
        kl = klass[p]
        for k in range(1, classes):
            perm = jnp.where(kl == k, table_ref[p, k], perm)
        st = fill[p]
        cond = perm * jnp.where(st == 0, 1.0, jnp.where(st == 1, 0.5, 0.25))
        conds.append(cond)
        turned.append(cond.T)
        fields.append(pressure[p].T)
        for side, at in ((0, 0), (1, width - 1)):
            halo_out[side, p : p + 1, :] = turned[p][at : at + 1]
            halo_out[side, plies + p : plies + p + 1, :] = fields[p][at : at + 1]

    pl.semaphore_wait(barrier, ns + nc - 2)
    ahead, behind = lax.rem(me_c + 1, nc), lax.rem(me_c + nc - 1, nc)
    halos = [
        pltpu.make_async_remote_copy(
            halo_out.at[side], halo_in.at[side], halo_send.at[side], halo_recv.at[side],
            {"chord": to}, MESH,
        )
        for side, to in ((0, behind), (1, ahead))
    ]
    for copy in halos:
        copy.start()

    def keeper(ref, p):
        def keep(k, al, be):
            ref[k, 0, p] = al
            ref[k, 1, p] = be

        return keep

    def kept(ref, p):
        return lambda k: (ref[k, 0, p], ref[k, 1, p])

    for p in range(plies):
        A, C, re = factor(conds[p], keeper(keep_s, p))
        A_s[p], C_s[p], E_s[p] = A, C, re
        put_coefs(coef_s, me_s, plies, p, A, C, conds[p])
    span_coefs = Gather("span", ns, me_s, coef_s, cs_send, cs_recv)
    span_coefs.start()

    row_id = lax.broadcasted_iota(jnp.int32, (rows, span_ref.shape[1]), 0) + me_s * rows
    col_id = lax.broadcasted_iota(jnp.int32, (width, span_ref.shape[1]), 0) + me_c * width
    row_hits = jnp.where(row_id == span_ref[...], rate_ref[...], 0.0)
    col_hits = jnp.where(col_id == chord_ref[...], 1.0, 0.0)
    plane = lax.dot_general(
        row_hits, col_hits, (((1,), (1,)), ((), ())),
        precision=lax.Precision.HIGHEST, preferred_element_type=jnp.float32,
    )

    explicit = []
    for p in range(plies):
        f, other = fields[p], fields[plies - 1 - p]
        g = HALF_RATE * (turned[p] + up(turned[p], 1))
        flow = to_row(1, g * (up(f, 1) - f), jnp.zeros_like(f))
        back = from_row(1, down(flow, 1), jnp.zeros_like(f))
        explicit.append(f + (flow - back) + COUPLE * (other - f))

    for p in range(plies):
        rhs = explicit[p].T + plane
        half[p] = rhs
        d = reduce_rhs(rhs, kept(keep_s, p), E_s[p])
        edge_s[me_s, p : p + 1, :] = d[:1]
        edge_s[me_s, plies + p : plies + p + 1, :] = d[rows - 1 :]
        for q, response in enumerate((A_s[p].T, C_s[p].T)):
            sides[2 * q, p : p + 1, :] = response[:1]
            sides[2 * q + 1, p : p + 1, :] = response[width - 1 :]

    for copy in halos:
        copy.wait_recv()

    def inflow(mine, theirs):
        conds_sum = halo_in[theirs, :plies, :] + halo_out[mine, :plies, :]
        return HALF_RATE * conds_sum * (halo_in[theirs, plies:, :] - halo_out[mine, plies:, :])

    first = jnp.where(me_c > 0, inflow(0, 1), 0.0)
    last = jnp.where(me_c < nc - 1, inflow(1, 0), 0.0)
    lane = lax.broadcasted_iota(jnp.int32, (plies, width), 1)
    for q in range(2):
        by_first = jnp.sum(sides[2 * q] * first, axis=1, keepdims=True)
        by_last = jnp.sum(sides[2 * q + 1] * last, axis=1, keepdims=True)
        edge_s[me_s, q * plies : (q + 1) * plies, :] = (
            edge_s[me_s, q * plies : (q + 1) * plies, :]
            + jnp.where(lane == 0, by_first, 0.0)
            + jnp.where(lane == width - 1, by_last, 0.0)
        )
    span_edges = Gather("span", ns, me_s, edge_s, es_send, es_recv)
    span_edges.start()

    lanes = lax.broadcasted_iota(jnp.int32, (width, rows), 0)
    for p in range(plies):
        change = jnp.where(lanes == 0, first[p : p + 1], 0.0) + jnp.where(
            lanes == width - 1, last[p : p + 1], 0.0
        )
        rhs = half[p] + change.T
        half[p] = rhs
        D[p] = reduce_rhs(rhs, kept(keep_s, p), E_s[p])

    for p in range(plies):
        A, C, re = factor(turned[p], keeper(keep_c, p))
        A_c[p], C_c[p], E_c[p] = A, C, re
        put_coefs(coef_c, me_c, plies, p, A, C, turned[p])
    chord_coefs = Gather("chord", nc, me_c, coef_c, cc_send, cc_recv)
    chord_coefs.start()

    span_coefs.wait()
    parts = flux_factor(coef_s, ns, plies)
    span_edges.wait()
    top, bottom = flux_solve(edge_s, ns, plies, me_s, *parts)
    stars = [D[p] + A_s[p] * top[p : p + 1] - C_s[p] * bottom[p : p + 1] for p in range(plies)]
    for p in range(plies):
        star, other = stars[p], stars[plies - 1 - p]
        second = 2.0 * star - half[p] + COUPLE * (other - star) + plane
        d = reduce_rhs(second.T, kept(keep_c, p), E_c[p])
        D_c[p] = d
        edge_c[me_c, p : p + 1, :] = d[:1]
        edge_c[me_c, plies + p : plies + p + 1, :] = d[width - 1 :]
    chord_edges = Gather("chord", nc, me_c, edge_c, ec_send, ec_recv)
    chord_edges.start()

    chord_coefs.wait()
    parts = flux_factor(coef_c, nc, plies)
    chord_edges.wait()
    top, bottom = flux_solve(edge_c, nc, plies, me_c, *parts)
    for p in range(plies):
        line = D_c[p] + A_c[p] * top[p : p + 1] - C_c[p] * bottom[p : p + 1]
        out_ref[p] = line.T

    for copy in halos:
        copy.wait_send()
    for gather in (span_coefs, chord_coefs, span_edges, chord_edges):
        gather.wait_sent()


def levels(n):
    return max(1, (n - 1).bit_length())


def per_device(ns, nc, pressure, fill_state, perm_class, perm_table, inlet_span, inlet_chord, inlet_rate):
    plies, rows, width = pressure.shape
    classes = perm_table.shape[1]
    inlets = inlet_span.shape[0]
    vmem = pl.BlockSpec(memory_space=pltpu.VMEM)
    hbm = pl.BlockSpec(memory_space=pltpu.HBM)
    f32 = jnp.float32
    block = pltpu.VMEM((plies, rows, width), f32)
    block_t = pltpu.VMEM((plies, width, rows), f32)
    iblock = pltpu.VMEM((plies, rows, width), jnp.int32)
    dma = lambda n: pltpu.SemaphoreType.DMA((n,))
    return pl.pallas_call(
        functools.partial(kernel, ns, nc, plies, classes),
        out_shape=pltpu.VMEM(pressure.shape, f32),
        in_specs=[hbm] * 7,
        out_specs=vmem,
        scratch_shapes=[
            block, iblock, iblock,
            pltpu.SMEM(perm_table.shape, f32),
            pltpu.VMEM((1, inlets), jnp.int32), pltpu.VMEM((1, inlets), jnp.int32), pltpu.VMEM((1, inlets), f32),
            block,
            pltpu.VMEM((levels(rows), 2, plies, rows, width), f32),
            pltpu.VMEM((levels(width), 2, plies, width, rows), f32),
            block, block, block, block_t, block_t, block_t, block, block_t,
            pltpu.VMEM((4, plies, rows), f32),
            pltpu.VMEM((2, 2 * plies, rows), f32),
            pltpu.VMEM((2, 2 * plies, rows), f32),
            pltpu.VMEM((ns, 5 * plies, width), f32),
            pltpu.VMEM((nc, 5 * plies, rows), f32),
            pltpu.VMEM((ns, 2 * plies, width), f32),
            pltpu.VMEM((nc, 2 * plies, rows), f32),
            dma(7), dma(2), dma(2),
            dma(ns), dma(ns), dma(nc), dma(nc), dma(ns), dma(ns), dma(nc), dma(nc),
        ],
        compiler_params=pltpu.CompilerParams(collective_id=0, has_side_effects=True, vmem_limit_bytes=LIMIT),
    )(
        *(
            pltpu.with_memory_space_constraint(x, pltpu.HBM)
            for x in (
                pressure, fill_state, perm_class, perm_table, inlet_span.reshape(1, inlets),
                inlet_chord.reshape(1, inlets), inlet_rate.reshape(1, inlets),
            )
        )
    )


def solution(mesh):
    block = P(None, "span", "chord")
    return jax.shard_map(
        functools.partial(per_device, mesh.shape["span"], mesh.shape["chord"]),
        mesh=mesh,
        in_specs=(block, block, block, P(), P(), P(), P()),
        out_specs=block,
        check_vma=False,
    )
```

```python
import functools

import jax
import jax.numpy as jnp
from jax import lax
from jax.experimental import pallas as pl
from jax.experimental.pallas import tpu as pltpu
from jax.sharding import PartitionSpec as P

HALF_RATE = 200.0
COUPLE = 0.3
MESH = pl.DeviceIdType.MESH
TILE = 8
LIMIT = 16 << 20


def down(x, s):
    if s % TILE == 0:
        return jnp.concatenate([x[-s:], x[:-s]], axis=0)
    return pltpu.roll(x, s, 0)


def up(x, s):
    if s % TILE == 0:
        return jnp.concatenate([x[s:], x[:s]], axis=0)
    return pltpu.roll(x, x.shape[0] - s, 0)


def from_row(s, value, other):
    if s % TILE == 0:
        return jnp.concatenate([other[:s], value[s:]], axis=0)
    rows = lax.broadcasted_iota(jnp.int32, value.shape, 0)
    return jnp.where(rows >= s, value, other)


def to_row(s, value, other):
    n = value.shape[0]
    if s % TILE == 0:
        return jnp.concatenate([value[: n - s], other[n - s :]], axis=0)
    rows = lax.broadcasted_iota(jnp.int32, value.shape, 0)
    return jnp.where(rows < n - s, value, other)


def factor(cond, keep):
    n = cond.shape[0]
    zero = jnp.zeros_like(cond)
    one = jnp.ones_like(cond)
    g = HALF_RATE * (cond + up(cond, 1))
    a = from_row(1, down(g, 1), one)
    c = to_row(1, g, one)
    e = one
    s, k = 1, 0
    while s < n:
        a_in = from_row(s, a, zero)
        c_in = to_row(s, c, zero)
        rb = 1.0 / (e + a_in + c_in)
        al = a_in * down(rb, s)
        be = c_in * up(rb, s)
        keep(k, al, be)
        a = from_row(s, al * down(a, s), a)
        c = to_row(s, be * up(c, s), c)
        e = e + al * down(e, s) + be * up(e, s)
        s, k = 2 * s, k + 1
    re = 1.0 / e
    return a * re, c * re, re


def reduce_rhs(d, kept, re):
    n = d.shape[0]
    s, k = 1, 0
    while s < n:
        al, be = kept(k)
        if s % TILE == 0:
            zero = jnp.zeros_like(d[:s])
            d = (
                d
                + jnp.concatenate([zero, al[s:] * d[:-s]], axis=0)
                + jnp.concatenate([be[:-s] * d[s:], zero], axis=0)
            )
        else:
            d = d + al * down(d, s) + be * up(d, s)
        s, k = 2 * s, k + 1
    return d * re


class Gather:
    def __init__(self, axis, n, me, buf, send, recv):
        self.copies = []
        self.landed = []
        for o in range(1, n):
            dst = lax.rem(me + o, n)
            src = lax.rem(me + n - o, n)
            self.copies.append(
                pltpu.make_async_remote_copy(
                    buf.at[me], buf.at[me], send.at[o], recv.at[o], {axis: dst}, MESH
                )
            )
            self.landed.append(
                pltpu.make_async_remote_copy(
                    buf.at[src], buf.at[src], send.at[o], recv.at[o], {axis: dst}, MESH
                )
            )

    def start(self):
        for copy in self.copies:
            copy.start()

    def wait(self):
        for copy in self.landed:
            copy.wait_recv()

    def wait_sent(self):
        for copy in self.copies:
            copy.wait_send()


def put_coefs(buf, me, plies, p, A, C, cond):
    n = A.shape[0]
    values = (A[:1], C[n - 1 :], A[n - 1 :], cond[:1], cond[n - 1 :])
    for q, v in enumerate(values):
        buf[me, q * plies + p : q * plies + p + 1, :] = v


def flux_factor(buf, n, plies):
    def at(j, q):
        return buf[j, q * plies : (q + 1) * plies, :]

    w, m = [None] * (n + 1), [None] * (n + 1)
    cross = [at(j, 2) for j in range(n)]
    for j in range(1, n):
        diag = 1.0 / (HALF_RATE * (at(j - 1, 4) + at(j, 3))) + at(j - 1, 1) + at(j, 0)
        if j > 1:
            m[j] = cross[j - 1] * w[j - 1]
            diag = diag - cross[j - 1] * m[j]
        w[j] = 1.0 / diag
    return w, m, cross


def flux_solve(buf, n, plies, me, w, m, cross):
    y = [None] * (n + 1)
    for j in range(1, n):
        r = buf[j - 1, plies : 2 * plies, :] - buf[j, :plies, :]
        y[j] = r if j == 1 else r + m[j] * y[j - 1]
    zero = jnp.zeros((plies, buf.shape[-1]), jnp.float32)
    top, bottom = zero, zero
    flux = None
    for j in range(n - 1, 0, -1):
        flux = w[j] * (y[j] if flux is None else y[j] + cross[j] * flux)
        top = jnp.where(me == j, flux, top)
        bottom = jnp.where(me + 1 == j, flux, bottom)
    return top, bottom


def kernel(
    ns, nc, plies, classes,
    pressure_hbm, fill_hbm, class_hbm, table_hbm, span_hbm, chord_hbm, rate_hbm,
    D_c, A_c, C_c, flux_ref,
    pressure, fill, klass, table_ref, span_ref, chord_ref, rate_ref, half, keep_s, keep_c, A_s, C_s, E_s, E_c, D, sides,
    halo_out, halo_in, coef_s, coef_c, edge_s, edge_c,
    load_sem, halo_send, halo_recv,
    cs_send, cs_recv, cc_send, cc_recv, es_send, es_recv, ec_send, ec_recv,
):
    rows, width = pressure.shape[1:]
    me_s, me_c = lax.axis_index("span"), lax.axis_index("chord")
    barrier = pltpu.get_barrier_semaphore()
    for o in range(1, nc):
        pl.semaphore_signal(
            barrier, inc=1, device_id={"chord": lax.rem(me_c + o, nc)}, device_id_type=MESH
        )
    loads = [
        pltpu.make_async_copy(src, dst, load_sem.at[i])
        for i, (src, dst) in enumerate(
            (
                (class_hbm, klass), (fill_hbm, fill), (pressure_hbm, pressure), (table_hbm, table_ref),
                (span_hbm, span_ref), (chord_hbm, chord_ref), (rate_hbm, rate_ref),
            )
        )
    ]
    for load in loads:
        load.start()
    for o in range(1, ns):
        pl.semaphore_signal(
            barrier, inc=1, device_id={"span": lax.rem(me_s + o, ns)}, device_id_type=MESH
        )

    for load in loads:
        load.wait()

    conds, turned, fields = [], [], []
    for p in range(plies):
        perm = jnp.full((rows, width), table_ref[p, 0], jnp.float32)
        kl = klass[p]
        for k in range(1, classes):
            perm = jnp.where(kl == k, table_ref[p, k], perm)
        st = fill[p]
        cond = perm * jnp.where(st == 0, 1.0, jnp.where(st == 1, 0.5, 0.25))
        conds.append(cond)
        turned.append(cond.T)
        fields.append(pressure[p].T)
        for side, at in ((0, 0), (1, width - 1)):
            halo_out[side, p : p + 1, :] = turned[p][at : at + 1]
            halo_out[side, plies + p : plies + p + 1, :] = fields[p][at : at + 1]

    pl.semaphore_wait(barrier, ns + nc - 2)
    ahead, behind = lax.rem(me_c + 1, nc), lax.rem(me_c + nc - 1, nc)
    halos = [
        pltpu.make_async_remote_copy(
            halo_out.at[side], halo_in.at[side], halo_send.at[side], halo_recv.at[side],
            {"chord": to}, MESH,
        )
        for side, to in ((0, behind), (1, ahead))
    ]
    for copy in halos:
        copy.start()

    def keeper(ref, p):
        def keep(k, al, be):
            ref[k, 0, p] = al
            ref[k, 1, p] = be

        return keep

    def kept(ref, p):
        return lambda k: (ref[k, 0, p], ref[k, 1, p])

    for p in range(plies):
        A, C, re = factor(conds[p], keeper(keep_s, p))
        A_s[p], C_s[p], E_s[p] = A, C, re
        put_coefs(coef_s, me_s, plies, p, A, C, conds[p])
    span_coefs = Gather("span", ns, me_s, coef_s, cs_send, cs_recv)
    span_coefs.start()

    row_id = lax.broadcasted_iota(jnp.int32, (rows, span_ref.shape[1]), 0) + me_s * rows
    col_id = lax.broadcasted_iota(jnp.int32, (width, span_ref.shape[1]), 0) + me_c * width
    row_hits = jnp.where(row_id == span_ref[...], rate_ref[...], 0.0)
    col_hits = jnp.where(col_id == chord_ref[...], 1.0, 0.0)
    plane = lax.dot_general(
        row_hits, col_hits, (((1,), (1,)), ((), ())),
        precision=lax.Precision.HIGHEST, preferred_element_type=jnp.float32,
    )

    explicit = []
    for p in range(plies):
        f, other = fields[p], fields[plies - 1 - p]
        g = HALF_RATE * (turned[p] + up(turned[p], 1))
        flow = to_row(1, g * (up(f, 1) - f), jnp.zeros_like(f))
        back = from_row(1, down(flow, 1), jnp.zeros_like(f))
        explicit.append(f + (flow - back) + COUPLE * (other - f))

    for p in range(plies):
        rhs = explicit[p].T + plane
        half[p] = rhs
        d = reduce_rhs(rhs, kept(keep_s, p), E_s[p])
        edge_s[me_s, p : p + 1, :] = d[:1]
        edge_s[me_s, plies + p : plies + p + 1, :] = d[rows - 1 :]
        for q, response in enumerate((A_s[p].T, C_s[p].T)):
            sides[2 * q, p : p + 1, :] = response[:1]
            sides[2 * q + 1, p : p + 1, :] = response[width - 1 :]

    for copy in halos:
        copy.wait_recv()

    def inflow(mine, theirs):
        conds_sum = halo_in[theirs, :plies, :] + halo_out[mine, :plies, :]
        return HALF_RATE * conds_sum * (halo_in[theirs, plies:, :] - halo_out[mine, plies:, :])

    first = jnp.where(me_c > 0, inflow(0, 1), 0.0)
    last = jnp.where(me_c < nc - 1, inflow(1, 0), 0.0)
    lane = lax.broadcasted_iota(jnp.int32, (plies, width), 1)
    for q in range(2):
        by_first = jnp.sum(sides[2 * q] * first, axis=1, keepdims=True)
        by_last = jnp.sum(sides[2 * q + 1] * last, axis=1, keepdims=True)
        edge_s[me_s, q * plies : (q + 1) * plies, :] = (
            edge_s[me_s, q * plies : (q + 1) * plies, :]
            + jnp.where(lane == 0, by_first, 0.0)
            + jnp.where(lane == width - 1, by_last, 0.0)
        )
    span_edges = Gather("span", ns, me_s, edge_s, es_send, es_recv)
    span_edges.start()

    lanes = lax.broadcasted_iota(jnp.int32, (width, rows), 0)
    for p in range(plies):
        change = jnp.where(lanes == 0, first[p : p + 1], 0.0) + jnp.where(
            lanes == width - 1, last[p : p + 1], 0.0
        )
        rhs = half[p] + change.T
        half[p] = rhs
        D[p] = reduce_rhs(rhs, kept(keep_s, p), E_s[p])

    for p in range(plies):
        A, C, re = factor(turned[p], keeper(keep_c, p))
        A_c[p], C_c[p], E_c[p] = A, C, re
        put_coefs(coef_c, me_c, plies, p, A, C, turned[p])
    chord_coefs = Gather("chord", nc, me_c, coef_c, cc_send, cc_recv)
    chord_coefs.start()

    span_coefs.wait()
    parts = flux_factor(coef_s, ns, plies)
    span_edges.wait()
    top, bottom = flux_solve(edge_s, ns, plies, me_s, *parts)
    stars = [D[p] + A_s[p] * top[p : p + 1] - C_s[p] * bottom[p : p + 1] for p in range(plies)]
    for p in range(plies):
        star, other = stars[p], stars[plies - 1 - p]
        second = 2.0 * star - half[p] + COUPLE * (other - star) + plane
        d = reduce_rhs(second.T, kept(keep_c, p), E_c[p])
        D_c[p] = d
        edge_c[me_c, p : p + 1, :] = d[:1]
        edge_c[me_c, plies + p : plies + p + 1, :] = d[width - 1 :]
    chord_edges = Gather("chord", nc, me_c, edge_c, ec_send, ec_recv)
    chord_edges.start()

    chord_coefs.wait()
    parts = flux_factor(coef_c, nc, plies)
    for copy in halos:
        copy.wait_send()
    for gather in (span_coefs, chord_coefs, span_edges):
        gather.wait_sent()
    chord_edges.wait()
    flux_ref[0], flux_ref[1] = flux_solve(edge_c, nc, plies, me_c, *parts)
    chord_edges.wait_sent()


def finish(plies, D_c, A_c, C_c, flux_ref, out_hbm, block, sem):
    copies = []
    for p in range(plies):
        top, bottom = flux_ref[0, p : p + 1, :], flux_ref[1, p : p + 1, :]
        block[p] = (D_c[p] + A_c[p] * top - C_c[p] * bottom).T
        copies.append(pltpu.make_async_copy(block.at[p], out_hbm.at[p], sem.at[p]))
        copies[-1].start()
    for copy in copies:
        copy.wait()


def levels(n):
    return max(1, (n - 1).bit_length())


def per_device(ns, nc, pressure, fill_state, perm_class, perm_table, inlet_span, inlet_chord, inlet_rate):
    plies, rows, width = pressure.shape
    classes = perm_table.shape[1]
    inlets = inlet_span.shape[0]
    vmem = pl.BlockSpec(memory_space=pltpu.VMEM)
    hbm = pl.BlockSpec(memory_space=pltpu.HBM)
    f32 = jnp.float32
    block = pltpu.VMEM((plies, rows, width), f32)
    block_t = pltpu.VMEM((plies, width, rows), f32)
    iblock = pltpu.VMEM((plies, rows, width), jnp.int32)
    dma = lambda n: pltpu.SemaphoreType.DMA((n,))
    lines = pltpu.VMEM((plies, width, rows), f32)
    solved = pl.pallas_call(
        functools.partial(kernel, ns, nc, plies, classes),
        out_shape=(lines, lines, lines, pltpu.VMEM((2, plies, rows), f32)),
        in_specs=[hbm] * 7,
        out_specs=(vmem,) * 4,
        scratch_shapes=[
            block, iblock, iblock,
            pltpu.SMEM(perm_table.shape, f32),
            pltpu.VMEM((1, inlets), jnp.int32), pltpu.VMEM((1, inlets), jnp.int32), pltpu.VMEM((1, inlets), f32),
            block,
            pltpu.VMEM((levels(rows), 2, plies, rows, width), f32),
            pltpu.VMEM((levels(width), 2, plies, width, rows), f32),
            block, block, block, block_t, block,
            pltpu.VMEM((4, plies, rows), f32),
            pltpu.VMEM((2, 2 * plies, rows), f32),
            pltpu.VMEM((2, 2 * plies, rows), f32),
            pltpu.VMEM((ns, 5 * plies, width), f32),
            pltpu.VMEM((nc, 5 * plies, rows), f32),
            pltpu.VMEM((ns, 2 * plies, width), f32),
            pltpu.VMEM((nc, 2 * plies, rows), f32),
            dma(7), dma(2), dma(2),
            dma(ns), dma(ns), dma(nc), dma(nc), dma(ns), dma(ns), dma(nc), dma(nc),
        ],
        compiler_params=pltpu.CompilerParams(collective_id=0, has_side_effects=True, vmem_limit_bytes=LIMIT),
    )(
        *(
            pltpu.with_memory_space_constraint(x, pltpu.HBM)
            for x in (
                pressure, fill_state, perm_class, perm_table, inlet_span.reshape(1, inlets),
                inlet_chord.reshape(1, inlets), inlet_rate.reshape(1, inlets),
            )
        )
    )
    return pl.pallas_call(
        functools.partial(finish, plies),
        out_shape=jax.ShapeDtypeStruct(pressure.shape, f32),
        in_specs=[vmem] * 4,
        out_specs=hbm,
        scratch_shapes=[block, dma(plies)],
        compiler_params=pltpu.CompilerParams(vmem_limit_bytes=LIMIT),
    )(*solved)


def solution(mesh):
    block = P(None, "span", "chord")
    return jax.shard_map(
        functools.partial(per_device, mesh.shape["span"], mesh.shape["chord"]),
        mesh=mesh,
        in_specs=(block, block, block, P(), P(), P(), P()),
        out_specs=block,
        check_vma=False,
    )
```

```python
import functools

import jax
import jax.numpy as jnp
from jax import lax
from jax.experimental import pallas as pl
from jax.experimental.pallas import tpu as pltpu
from jax.sharding import PartitionSpec as P

HALF_RATE = 200.0
COUPLE = 0.3
MESH = pl.DeviceIdType.MESH
TILE = 8
LIMIT = 16 << 20


def down(x, s):
    if s % TILE == 0:
        return jnp.concatenate([x[-s:], x[:-s]], axis=0)
    return pltpu.roll(x, s, 0)


def up(x, s):
    if s % TILE == 0:
        return jnp.concatenate([x[s:], x[:s]], axis=0)
    return pltpu.roll(x, x.shape[0] - s, 0)


def from_row(s, value, other):
    if s % TILE == 0:
        return jnp.concatenate([other[:s], value[s:]], axis=0)
    rows = lax.broadcasted_iota(jnp.int32, value.shape, 0)
    return jnp.where(rows >= s, value, other)


def to_row(s, value, other):
    n = value.shape[0]
    if s % TILE == 0:
        return jnp.concatenate([value[: n - s], other[n - s :]], axis=0)
    rows = lax.broadcasted_iota(jnp.int32, value.shape, 0)
    return jnp.where(rows < n - s, value, other)


def factor(cond, keep):
    n = cond.shape[0]
    zero = jnp.zeros_like(cond)
    one = jnp.ones_like(cond)
    g = HALF_RATE * (cond + up(cond, 1))
    a = from_row(1, down(g, 1), one)
    c = to_row(1, g, one)
    e = one
    s, k = 1, 0
    while s < n:
        a_in = from_row(s, a, zero)
        c_in = to_row(s, c, zero)
        rb = 1.0 / (e + a_in + c_in)
        al = a_in * down(rb, s)
        be = c_in * up(rb, s)
        keep(k, al, be)
        a = from_row(s, al * down(a, s), a)
        c = to_row(s, be * up(c, s), c)
        e = e + al * down(e, s) + be * up(e, s)
        s, k = 2 * s, k + 1
    re = 1.0 / e
    return a * re, c * re, re


def reduce_rhs(d, kept, re):
    n = d.shape[0]
    s, k = 1, 0
    while s < n:
        al, be = kept(k)
        if s % TILE == 0:
            zero = jnp.zeros_like(d[:s])
            d = (
                d
                + jnp.concatenate([zero, al[s:] * d[:-s]], axis=0)
                + jnp.concatenate([be[:-s] * d[s:], zero], axis=0)
            )
        else:
            d = d + al * down(d, s) + be * up(d, s)
        s, k = 2 * s, k + 1
    return d * re


class Gather:
    def __init__(self, axis, n, me, buf, send, recv):
        self.copies = []
        self.landed = []
        for o in range(1, n):
            dst = lax.rem(me + o, n)
            src = lax.rem(me + n - o, n)
            self.copies.append(
                pltpu.make_async_remote_copy(
                    buf.at[me], buf.at[me], send.at[o], recv.at[o], {axis: dst}, MESH
                )
            )
            self.landed.append(
                pltpu.make_async_remote_copy(
                    buf.at[src], buf.at[src], send.at[o], recv.at[o], {axis: dst}, MESH
                )
            )

    def start(self):
        for copy in self.copies:
            copy.start()

    def wait(self):
        for copy in self.landed:
            copy.wait_recv()

    def wait_sent(self):
        for copy in self.copies:
            copy.wait_send()


def put_coefs(buf, me, plies, p, A, C, cond):
    n = A.shape[0]
    values = (A[:1], C[n - 1 :], A[n - 1 :], cond[:1], cond[n - 1 :])
    for q, v in enumerate(values):
        buf[me, q * plies + p : q * plies + p + 1, :] = v


def flux_factor(buf, n, plies):
    def at(j, q):
        return buf[j, q * plies : (q + 1) * plies, :]

    w, m = [None] * (n + 1), [None] * (n + 1)
    cross = [at(j, 2) for j in range(n)]
    for j in range(1, n):
        diag = 1.0 / (HALF_RATE * (at(j - 1, 4) + at(j, 3))) + at(j - 1, 1) + at(j, 0)
        if j > 1:
            m[j] = cross[j - 1] * w[j - 1]
            diag = diag - cross[j - 1] * m[j]
        w[j] = 1.0 / diag
    return w, m, cross


def flux_solve(buf, n, plies, me, w, m, cross):
    y = [None] * (n + 1)
    for j in range(1, n):
        r = buf[j - 1, plies : 2 * plies, :] - buf[j, :plies, :]
        y[j] = r if j == 1 else r + m[j] * y[j - 1]
    zero = jnp.zeros((plies, buf.shape[-1]), jnp.float32)
    top, bottom = zero, zero
    flux = None
    for j in range(n - 1, 0, -1):
        flux = w[j] * (y[j] if flux is None else y[j] + cross[j] * flux)
        top = jnp.where(me == j, flux, top)
        bottom = jnp.where(me + 1 == j, flux, bottom)
    return top, bottom


def kernel(
    ns, nc, plies, classes,
    pressure_hbm, fill_hbm, class_hbm, table_hbm, span_hbm, chord_hbm, rate_hbm,
    D_c, A_c, C_c, flux_ref,
    pressure, fill, klass, table_ref, span_ref, chord_ref, rate_ref, half, keep_s, keep_c, A_s, C_s, E_s, E_c, D, sides,
    halo_out, halo_in, coef_s, coef_c, edge_s, edge_c,
    load_sem, halo_send, halo_recv,
    cs_send, cs_recv, cc_send, cc_recv, es_send, es_recv, ec_send, ec_recv,
):
    rows, width = pressure.shape[1:]
    me_s, me_c = lax.axis_index("span"), lax.axis_index("chord")
    barrier = pltpu.get_barrier_semaphore()
    for o in range(1, nc):
        pl.semaphore_signal(
            barrier, inc=1, device_id={"chord": lax.rem(me_c + o, nc)}, device_id_type=MESH
        )
    loads = [
        pltpu.make_async_copy(src, dst, load_sem.at[i])
        for i, (src, dst) in enumerate(
            (
                (class_hbm, klass), (fill_hbm, fill), (pressure_hbm, pressure), (table_hbm, table_ref),
                (span_hbm, span_ref), (chord_hbm, chord_ref), (rate_hbm, rate_ref),
            )
        )
    ]
    for load in loads:
        load.start()
    for o in range(1, ns):
        pl.semaphore_signal(
            barrier, inc=1, device_id={"span": lax.rem(me_s + o, ns)}, device_id_type=MESH
        )

    for i in (0, 1, 3):
        loads[i].wait()

    conds, turned, fields = [], [], []
    for p in range(plies):
        perm = jnp.full((rows, width), table_ref[p, 0], jnp.float32)
        kl = klass[p]
        for k in range(1, classes):
            perm = jnp.where(kl == k, table_ref[p, k], perm)
        st = fill[p]
        cond = perm * jnp.where(st == 0, 1.0, jnp.where(st == 1, 0.5, 0.25))
        conds.append(cond)
        turned.append(cond.T)
        if p == 0:
            loads[2].wait()
        fields.append(pressure[p].T)
        for side, at in ((0, 0), (1, width - 1)):
            halo_out[side, p : p + 1, :] = turned[p][at : at + 1]
            halo_out[side, plies + p : plies + p + 1, :] = fields[p][at : at + 1]

    pl.semaphore_wait(barrier, ns + nc - 2)
    ahead, behind = lax.rem(me_c + 1, nc), lax.rem(me_c + nc - 1, nc)
    halos = [
        pltpu.make_async_remote_copy(
            halo_out.at[side], halo_in.at[side], halo_send.at[side], halo_recv.at[side],
            {"chord": to}, MESH,
        )
        for side, to in ((0, behind), (1, ahead))
    ]
    for copy in halos:
        copy.start()

    def keeper(ref, p):
        def keep(k, al, be):
            ref[k, 0, p] = al
            ref[k, 1, p] = be

        return keep

    def kept(ref, p):
        return lambda k: (ref[k, 0, p], ref[k, 1, p])

    for p in range(plies):
        A, C, re = factor(conds[p], keeper(keep_s, p))
        A_s[p], C_s[p], E_s[p] = A, C, re
        put_coefs(coef_s, me_s, plies, p, A, C, conds[p])
    span_coefs = Gather("span", ns, me_s, coef_s, cs_send, cs_recv)
    span_coefs.start()

    for load in loads[4:]:
        load.wait()
    row_id = lax.broadcasted_iota(jnp.int32, (rows, span_ref.shape[1]), 0) + me_s * rows
    col_id = lax.broadcasted_iota(jnp.int32, (width, span_ref.shape[1]), 0) + me_c * width
    row_hits = jnp.where(row_id == span_ref[...], rate_ref[...], 0.0)
    col_hits = jnp.where(col_id == chord_ref[...], 1.0, 0.0)
    plane = lax.dot_general(
        row_hits, col_hits, (((1,), (1,)), ((), ())),
        precision=lax.Precision.HIGHEST, preferred_element_type=jnp.float32,
    )

    explicit = []
    for p in range(plies):
        f, other = fields[p], fields[plies - 1 - p]
        g = HALF_RATE * (turned[p] + up(turned[p], 1))
        flow = to_row(1, g * (up(f, 1) - f), jnp.zeros_like(f))
        back = from_row(1, down(flow, 1), jnp.zeros_like(f))
        explicit.append(f + (flow - back) + COUPLE * (other - f))

    for p in range(plies):
        rhs = explicit[p].T + plane
        half[p] = rhs
        d = reduce_rhs(rhs, kept(keep_s, p), E_s[p])
        edge_s[me_s, p : p + 1, :] = d[:1]
        edge_s[me_s, plies + p : plies + p + 1, :] = d[rows - 1 :]
        for q, response in enumerate((A_s[p].T, C_s[p].T)):
            sides[2 * q, p : p + 1, :] = response[:1]
            sides[2 * q + 1, p : p + 1, :] = response[width - 1 :]

    for copy in halos:
        copy.wait_recv()

    def inflow(mine, theirs):
        conds_sum = halo_in[theirs, :plies, :] + halo_out[mine, :plies, :]
        return HALF_RATE * conds_sum * (halo_in[theirs, plies:, :] - halo_out[mine, plies:, :])

    first = jnp.where(me_c > 0, inflow(0, 1), 0.0)
    last = jnp.where(me_c < nc - 1, inflow(1, 0), 0.0)
    lane = lax.broadcasted_iota(jnp.int32, (plies, width), 1)
    for q in range(2):
        by_first = jnp.sum(sides[2 * q] * first, axis=1, keepdims=True)
        by_last = jnp.sum(sides[2 * q + 1] * last, axis=1, keepdims=True)
        edge_s[me_s, q * plies : (q + 1) * plies, :] = (
            edge_s[me_s, q * plies : (q + 1) * plies, :]
            + jnp.where(lane == 0, by_first, 0.0)
            + jnp.where(lane == width - 1, by_last, 0.0)
        )
    span_edges = Gather("span", ns, me_s, edge_s, es_send, es_recv)
    span_edges.start()

    lanes = lax.broadcasted_iota(jnp.int32, (width, rows), 0)
    for p in range(plies):
        change = jnp.where(lanes == 0, first[p : p + 1], 0.0) + jnp.where(
            lanes == width - 1, last[p : p + 1], 0.0
        )
        rhs = half[p] + change.T
        half[p] = rhs
        D[p] = reduce_rhs(rhs, kept(keep_s, p), E_s[p])

    for p in range(plies):
        A, C, re = factor(turned[p], keeper(keep_c, p))
        A_c[p], C_c[p], E_c[p] = A, C, re
        put_coefs(coef_c, me_c, plies, p, A, C, turned[p])
    chord_coefs = Gather("chord", nc, me_c, coef_c, cc_send, cc_recv)
    chord_coefs.start()

    span_coefs.wait()
    parts = flux_factor(coef_s, ns, plies)
    span_edges.wait()
    top, bottom = flux_solve(edge_s, ns, plies, me_s, *parts)
    stars = [D[p] + A_s[p] * top[p : p + 1] - C_s[p] * bottom[p : p + 1] for p in range(plies)]
    for p in range(plies):
        star, other = stars[p], stars[plies - 1 - p]
        second = 2.0 * star - half[p] + COUPLE * (other - star) + plane
        d = reduce_rhs(second.T, kept(keep_c, p), E_c[p])
        D_c[p] = d
        edge_c[me_c, p : p + 1, :] = d[:1]
        edge_c[me_c, plies + p : plies + p + 1, :] = d[width - 1 :]
    chord_edges = Gather("chord", nc, me_c, edge_c, ec_send, ec_recv)
    chord_edges.start()

    chord_coefs.wait()
    parts = flux_factor(coef_c, nc, plies)
    for copy in halos:
        copy.wait_send()
    for gather in (span_coefs, chord_coefs, span_edges):
        gather.wait_sent()
    chord_edges.wait()
    flux_ref[0], flux_ref[1] = flux_solve(edge_c, nc, plies, me_c, *parts)
    chord_edges.wait_sent()


def finish(plies, D_c, A_c, C_c, flux_ref, out_hbm, block, sem):
    copies = []
    for p in range(plies):
        top, bottom = flux_ref[0, p : p + 1, :], flux_ref[1, p : p + 1, :]
        block[p] = (D_c[p] + A_c[p] * top - C_c[p] * bottom).T
        copies.append(pltpu.make_async_copy(block.at[p], out_hbm.at[p], sem.at[p]))
        copies[-1].start()
    for copy in copies:
        copy.wait()


def levels(n):
    return max(1, (n - 1).bit_length())


def per_device(ns, nc, pressure, fill_state, perm_class, perm_table, inlet_span, inlet_chord, inlet_rate):
    plies, rows, width = pressure.shape
    classes = perm_table.shape[1]
    inlets = inlet_span.shape[0]
    vmem = pl.BlockSpec(memory_space=pltpu.VMEM)
    hbm = pl.BlockSpec(memory_space=pltpu.HBM)
    f32 = jnp.float32
    block = pltpu.VMEM((plies, rows, width), f32)
    block_t = pltpu.VMEM((plies, width, rows), f32)
    iblock = pltpu.VMEM((plies, rows, width), jnp.int32)
    dma = lambda n: pltpu.SemaphoreType.DMA((n,))
    lines = pltpu.VMEM((plies, width, rows), f32)
    solved = pl.pallas_call(
        functools.partial(kernel, ns, nc, plies, classes),
        out_shape=(lines, lines, lines, pltpu.VMEM((2, plies, rows), f32)),
        in_specs=[hbm] * 7,
        out_specs=(vmem,) * 4,
        scratch_shapes=[
            block, iblock, iblock,
            pltpu.SMEM(perm_table.shape, f32),
            pltpu.VMEM((1, inlets), jnp.int32), pltpu.VMEM((1, inlets), jnp.int32), pltpu.VMEM((1, inlets), f32),
            block,
            pltpu.VMEM((levels(rows), 2, plies, rows, width), f32),
            pltpu.VMEM((levels(width), 2, plies, width, rows), f32),
            block, block, block, block_t, block,
            pltpu.VMEM((4, plies, rows), f32),
            pltpu.VMEM((2, 2 * plies, rows), f32),
            pltpu.VMEM((2, 2 * plies, rows), f32),
            pltpu.VMEM((ns, 5 * plies, width), f32),
            pltpu.VMEM((nc, 5 * plies, rows), f32),
            pltpu.VMEM((ns, 2 * plies, width), f32),
            pltpu.VMEM((nc, 2 * plies, rows), f32),
            dma(7), dma(2), dma(2),
            dma(ns), dma(ns), dma(nc), dma(nc), dma(ns), dma(ns), dma(nc), dma(nc),
        ],
        compiler_params=pltpu.CompilerParams(collective_id=0, has_side_effects=True, vmem_limit_bytes=LIMIT),
    )(
        *(
            pltpu.with_memory_space_constraint(x, pltpu.HBM)
            for x in (
                pressure, fill_state, perm_class, perm_table, inlet_span.reshape(1, inlets),
                inlet_chord.reshape(1, inlets), inlet_rate.reshape(1, inlets),
            )
        )
    )
    return pl.pallas_call(
        functools.partial(finish, plies),
        out_shape=jax.ShapeDtypeStruct(pressure.shape, f32),
        in_specs=[vmem] * 4,
        out_specs=hbm,
        scratch_shapes=[block, dma(plies)],
        compiler_params=pltpu.CompilerParams(vmem_limit_bytes=LIMIT),
    )(*solved)


def solution(mesh):
    block = P(None, "span", "chord")
    return jax.shard_map(
        functools.partial(per_device, mesh.shape["span"], mesh.shape["chord"]),
        mesh=mesh,
        in_specs=(block, block, block, P(), P(), P(), P()),
        out_specs=block,
        check_vma=False,
    )
```
